256 devices in a mesh: wide: 32 (over z, x), narrow: 8 (over y, core).
Axes of the slice: x: 4, y: 4, z: 8, core: 2. Of those that a mesh axis runs over, the one named last changes fastest.
Arguments:
- walkers: bfloat16 [512, 768, 128], P('wide', 'narrow'), may hold values from -6 to 6
- intersection_inverse: bfloat16 [512, 128, 128], P('wide')
- noise: bfloat16 [512, 1024], P('wide'), may hold values from -6 to 6
- half_cholesky: bfloat16 [128, 768, 1024], P('wide', 'narrow'), may hold values from -0.25 to 0.25
- cholesky: bfloat16 [768, 768, 1024], P('narrow', 'wide'), may hold values from -0.1875 to 0.1875
- comb_source: int32 [512], P('wide'), may hold values from 0 to 511, as said below
Outputs:
- new_walkers: bfloat16 [512, 768, 128], P('wide', 'narrow')
- force_bias: float32 [512, 1024], P(('wide', 'narrow'))
The draws below stay inside these ranges and needn't reach their ends.
Inputs may be any that keep to these rules, and one draw needn't show every extreme that they name: comb_source[j] lies in the block of 16 slots that holds j or in one of the two blocks beside it; within each block the sources never fall; every block but the first copies some walker of the block before it, and every block but the last some walker of the block after it.
All inputs are finite; a program needn't handle non-finite values.
Results may differ from the reference program's by a relative error of at most 0.0085.
Values may be sent and summed in bfloat16 or wider, within the bound.
No kernel may reach another device: no remote copies, remote signals or barrier semaphores. Data moves between devices by JAX's collectives and lax.ppermute only.
A program may use at most 128 MiB of HBM per device.

```python
import math
import jax
import jax.numpy as jnp
from jax import lax

ORBITALS = 768
ELECTRONS = 128
VECTORS = 1024
WALK_DEV = 16
WALKERS = 512


def draw_intersection_inverse(key, part):
    inner_key = jax.random.fold_in(key, 11)
    shape_all = (WALKERS, ELECTRONS, ELECTRONS)
    spread = jax.random.normal(inner_key, shape_all, jnp.float32)
    identity = jnp.eye(ELECTRONS, dtype=jnp.float32)
    return (identity[None, :, :] + 0.5 * ELECTRONS ** (-0.5) * spread).astype(jnp.bfloat16)


def draw_comb_source(key, part):
    key_mid = jax.random.fold_in(key, 21)
    key_left = jax.random.fold_in(key, 22)
    key_right = jax.random.fold_in(key, 23)
    block_count = WALKERS // WALK_DEV
    slots = jnp.arange(WALKERS, dtype=jnp.int32)
    owner = slots // WALK_DEV
    within = slots % WALK_DEV
    low_edge = jnp.maximum(owner - 1, 0) * WALK_DEV
    high_edge = jnp.minimum(owner + 2, block_count) * WALK_DEV
    middle_draw = jax.random.randint(key_mid, (WALKERS,), 0, 1 << 30, jnp.int32)
    left_draw = jax.random.randint(key_left, (WALKERS,), 0, WALK_DEV, jnp.int32)
    right_draw = jax.random.randint(key_right, (WALKERS,), 0, WALK_DEV, jnp.int32)
    chosen = low_edge + middle_draw % (high_edge - low_edge)
    from_left = (owner - 1) * WALK_DEV + left_draw
    from_right = (owner + 1) * WALK_DEV + right_draw
    chosen = jnp.where((within == 0) & (owner > 0), from_left, chosen)
    chosen = jnp.where((within == WALK_DEV - 1) & (owner < block_count - 1), from_right, chosen)
    ordered = jnp.sort(chosen.reshape(block_count, WALK_DEV), axis=1)
    return ordered.reshape(WALKERS).astype(jnp.int32)


def shard_levels(stream_key, dims, cuts, least, top_value):
    def one(axis_at, blocks):
        heights = jax.random.uniform(jax.random.fold_in(jax.random.fold_in(stream_key, 6), axis_at), (blocks,), jnp.float32, least / len(cuts), top_value / len(cuts))
        return jnp.repeat(jnp.exp(heights), dims[axis_at] // blocks).reshape((-1,) + (1,) * (len(dims) - axis_at - 1))

    gain = one(*cuts[0])
    for cut in cuts[1:]:
        gain = gain * one(*cut)
    return gain


def gaussian(rng, shape, deviation, limit, cuts=(), kind=jnp.bfloat16):
    entries = deviation * jax.random.normal(rng, shape, jnp.float32)
    if cuts:
        entries = entries * shard_levels(rng, shape, cuts, -0.22, 0.18)
    return jnp.clip(entries, -limit, limit).astype(kind)


def setup_inputs(seed: int = 0) -> dict:
    key_of = jax.random.split(jax.random.key(seed), 7)
    return {
        "walkers": gaussian(key_of[0], (WALKERS, ORBITALS, ELECTRONS), 1.0, 6.0, ((0, 32), (1, 8))),
        "intersection_inverse": draw_intersection_inverse(jax.random.fold_in(key_of[6], 71), 0),
        "noise": gaussian(key_of[2], (WALKERS, VECTORS), 1.0, 6.0, ((0, 32),)),
        "half_cholesky": gaussian(key_of[3], (ELECTRONS, ORBITALS, VECTORS), (5.5 * (ORBITALS * ELECTRONS) ** -0.5), 0.25, ((0, 32), (1, 8))),
        "cholesky": gaussian(key_of[4], (ORBITALS, ORBITALS, VECTORS), (11.5 * (VECTORS * ORBITALS) ** -0.5), 0.1875, ((0, 8), (1, 32))),
        "comb_source": draw_comb_source(jax.random.fold_in(key_of[6], 71), 0),
    }


time_step = 0.01

def reference(walkers, intersection_inverse, noise, half_cholesky, cholesky, comb_source):
    rotated = jnp.einsum('wiq,wqp->wip', walkers.astype(jnp.float32), intersection_inverse.astype(jnp.float32), precision=lax.Precision.HIGHEST).astype(jnp.bfloat16)
    pair_rows = jnp.transpose(rotated, (0, 2, 1)).reshape(WALKERS, ELECTRONS * ORBITALS)
    force_bias = jnp.dot(pair_rows, half_cholesky.reshape(ELECTRONS * ORBITALS, VECTORS), preferred_element_type=jnp.float32)
    aux_field = (math.sqrt(time_step) * noise.astype(jnp.float32) + time_step * force_bias).astype(jnp.bfloat16)
    flat_chol = cholesky.reshape(ORBITALS * ORBITALS, VECTORS)
    field_blocks = aux_field.reshape(WALKERS // WALK_DEV, WALK_DEV, VECTORS)
    walker_blocks = walkers.reshape(WALKERS // WALK_DEV, WALK_DEV, ORBITALS, ELECTRONS)

    def propagate_block(pieces):
        field_block, walker_block = pieces
        op_block = jnp.dot(flat_chol, field_block.T, preferred_element_type=jnp.float32).astype(jnp.bfloat16)
        op_float = op_block.reshape(ORBITALS, ORBITALS, WALK_DEV).astype(jnp.float32)

        def apply_op(current):
            return jnp.einsum('ijw,wje->wie', op_float, current.astype(jnp.float32), precision=lax.Precision.HIGHEST)
        term_one = apply_op(walker_block).astype(jnp.bfloat16)
        term_two = (apply_op(term_one) / 2.0).astype(jnp.bfloat16)
        term_three = (apply_op(term_two) / 3.0).astype(jnp.bfloat16)
        term_four = apply_op(term_three) / 4.0
        summed = walker_block.astype(jnp.float32) + term_one.astype(jnp.float32) + term_two.astype(jnp.float32) + term_three.astype(jnp.float32) + term_four
        return summed.astype(jnp.bfloat16)
    propagated = lax.map(propagate_block, (field_blocks, walker_blocks)).reshape(WALKERS, ORBITALS, ELECTRONS)
    new_walkers = jnp.take(propagated, comb_source.astype(jnp.int32), axis=0)
    return (new_walkers, force_bias)
```

```python
import math

import jax
import jax.numpy as jnp
from jax import lax
from jax.sharding import Mesh, PartitionSpec as P

time_step = 0.01
WIDE = ("z", "x")
NARROW = ("y", "c")
ALL = WIDE + NARROW


def exchange(blocks, axes):
    return lax.all_to_all(blocks, axes, split_axis=0, concat_axis=0, tiled=True)


def slot_walkers(walkers, offset, wide_count):
    up = [(i, (i + 1) % wide_count) for i in range(wide_count - 1)]
    down = [(j, i) for i, j in up]
    before = lax.ppermute(walkers, WIDE, up)
    after = lax.ppermute(walkers, WIDE, down)
    padded = jnp.concatenate([before, walkers, after], axis=0)
    return jnp.take(padded, offset, axis=0)


def per_device(walkers, intersection_inverse, noise, half_cholesky, cholesky, comb_source):
    walk_local, row_count, electrons = walkers.shape
    col_count, vectors = cholesky.shape[1:]
    wide_count = lax.axis_size(WIDE)
    narrow_count = lax.axis_size(NARROW)
    share = walk_local // narrow_count
    wide_at = lax.axis_index(WIDE)
    narrow_at = lax.axis_index(NARROW)
    root_step = math.sqrt(time_step)
    f32, bf16 = jnp.float32, jnp.bfloat16

    offset = comb_source - (wide_at - 1) * walk_local
    chosen = slot_walkers(walkers, offset, wide_count)
    chosen = chosen.reshape(narrow_count, share, row_count, electrons)
    chosen = exchange(chosen, NARROW)
    current = chosen.transpose(1, 0, 2, 3).reshape(share, narrow_count * row_count, electrons)

    rotated = jnp.einsum(
        "wiq,wqp->wpi", walkers, intersection_inverse, preferred_element_type=f32
    ).astype(bf16)
    rotated = rotated.reshape(walk_local, wide_count, -1).transpose(1, 0, 2)
    pairs = exchange(rotated, WIDE).reshape(wide_count * walk_local, -1)
    partial = jnp.dot(pairs, half_cholesky.reshape(-1, vectors), preferred_element_type=f32)
    partial = partial.astype(bf16).reshape(wide_count, narrow_count, share, vectors)
    partial = exchange(partial.transpose(1, 0, 2, 3), NARROW)
    partial = jnp.sum(partial.astype(f32), axis=0).astype(bf16)
    partial = exchange(partial, WIDE)
    force_bias = jnp.sum(partial.astype(f32), axis=0)

    own_noise = lax.dynamic_slice_in_dim(noise, narrow_at * share, share, 0)
    aux = (root_step * own_noise.astype(f32) + time_step * force_bias).astype(bf16)
    own_offset = lax.dynamic_slice_in_dim(offset, narrow_at * share, share, 0).astype(bf16)
    aux = jnp.concatenate([aux, jnp.broadcast_to(own_offset[:, None], (share, 128))], axis=1)
    aux = exchange(jnp.broadcast_to(aux[None], (wide_count,) + aux.shape), WIDE)
    aux = exchange(jnp.broadcast_to(aux[None], (narrow_count,) + aux.shape), NARROW)
    offsets = aux[:, :, :, vectors].transpose(1, 0, 2).astype(jnp.int32)
    source = offsets + (jnp.arange(wide_count, dtype=jnp.int32)[:, None, None] - 1) * walk_local
    source = source.reshape(-1)
    block, inner = source // walk_local, source % walk_local
    row = (inner // share) * (wide_count * share) + block * share + inner % share
    table = aux[..., :vectors].reshape(-1, vectors)
    pick = (row[:, None] == jnp.arange(table.shape[0], dtype=jnp.int32)[None]).astype(bf16)
    fields = jnp.dot(pick, table, preferred_element_type=f32).astype(bf16)

    flat_chol = cholesky.reshape(row_count * col_count, vectors)
    operator = lax.dot_general(
        fields, flat_chol, (((1,), (1,)), ((), ())), preferred_element_type=f32
    ).astype(bf16)
    operator = exchange(operator.reshape(wide_count * narrow_count, share, -1), ALL)
    operator = operator.reshape(wide_count, narrow_count, share, row_count, col_count)
    orbitals = narrow_count * row_count
    operator = operator.transpose(2, 1, 3, 0, 4).reshape(share, orbitals, orbitals)
    summed = current.astype(f32)
    for degree in range(1, 5):
        product = jnp.einsum(
            "wij,wje->wie", operator, current, preferred_element_type=f32
        ) / float(degree)
        if degree < 4:
            current = product.astype(bf16)
            summed = summed + current.astype(f32)
        else:
            summed = summed + product
    propagated = summed.astype(bf16).reshape(share, narrow_count, row_count, electrons)
    new_walkers = exchange(propagated.transpose(1, 0, 2, 3), NARROW)
    return (new_walkers.reshape(walk_local, row_count, electrons), force_bias)


def solution(mesh):
    fine = Mesh(mesh.devices.reshape(8, 4, 4, 2), ALL)
    in_specs = (
        P(WIDE, NARROW, None),
        P(WIDE, None, None),
        P(WIDE, None),
        P(WIDE, NARROW, None),
        P(NARROW, WIDE, None),
        P(WIDE),
    )
    out_specs = (P(WIDE, NARROW, None), P(ALL, None))
    return jax.shard_map(
        per_device, mesh=fine, in_specs=in_specs, out_specs=out_specs, check_vma=False
    )
```

```python
import math

import jax
import jax.numpy as jnp
from jax import lax
from jax.experimental import pallas as pl
from jax.experimental.pallas import tpu as pltpu
from jax.sharding import Mesh, PartitionSpec as P

time_step = 0.01
WIDE = ("z", "x")
WIDE_X = ("x", "z")
NARROW = ("y", "c")
PLANE = ("x", "y", "c")
MIXED = ("x", "y", "c", "z")
ALL = WIDE + NARROW
LANES = 128


def exchange(blocks, axes):
    return lax.all_to_all(blocks, axes, split_axis=0, concat_axis=0, tiled=True)


def slot_walkers(walkers, offset, wide_count):
    up = [(i, (i + 1) % wide_count) for i in range(wide_count - 1)]
    down = [(j, i) for i, j in up]
    before = lax.ppermute(walkers, WIDE, up)
    after = lax.ppermute(walkers, WIDE, down)
    padded = jnp.concatenate([before, walkers, after], axis=0)
    return jnp.take(padded, offset, axis=0)


def packed_cholesky(cholesky):
    row_count, col_count, vectors = cholesky.shape
    by_col = cholesky.transpose(1, 0, 2)
    full = col_count * row_count // LANES
    rest = LANES - row_count
    tail = by_col[full:].reshape(full, rest, vectors)
    return jnp.concatenate([by_col[:full], tail], axis=1).reshape(full * LANES, vectors)


def propagate_kernel(blocks_ref, current_ref, out_ref, matrix_ref, term_ref, total_ref):
    share = blocks_ref.shape[0]
    f32, bf16 = jnp.float32, jnp.bfloat16
    lane = lax.broadcasted_iota(jnp.int32, (32, 128), 1)

    def assemble(s, carry):
        def rows_of(t, n):
            at = t * 128
            pieces = [
                blocks_ref[s, x * 64 + n * 8 : x * 64 + n * 8 + 8, at : at + 128]
                for x in range(4)
            ]
            return jnp.concatenate([piece.astype(f32) for piece in pieces], axis=0)

        for j in range(24):
            chunks = []
            for n in range(8):
                if j < 18:
                    chunk = rows_of(j, n)
                else:
                    q = 3 * (j - 18)
                    chunk = jnp.where(
                        lane < 32,
                        pltpu.roll(rows_of(q, n), 32, 1),
                        jnp.where(
                            lane < 64,
                            pltpu.roll(rows_of(q + 1, n), 64, 1),
                            pltpu.roll(rows_of(q + 2, n), 96, 1),
                        ),
                    )
                chunks.append(chunk)
            for half in range(2):
                first, second, third, fourth = chunks[4 * half : 4 * half + 4]
                second = pltpu.roll(second, 96, 1)
                third = pltpu.roll(third, 64, 1)
                fourth = pltpu.roll(fourth, 32, 1)
                tiles = (
                    jnp.where(lane < 96, first, second),
                    jnp.where(lane < 64, second, third),
                    jnp.where(lane < 32, third, fourth),
                )
                for k, tile in enumerate(tiles):
                    at = half * 384 + k * 128
                    matrix_ref[s, j * 32 : (j + 1) * 32, at : at + 128] = tile.astype(bf16)
        return carry

    lax.fori_loop(0, share, assemble, 0)
    for s in range(share):
        start = current_ref[s].astype(f32)
        term_ref[s] = start
        total_ref[s] = start
    for degree in range(1, 5):
        for s in range(share):
            rows = [
                term_ref[s, pl.ds(x * 24 + j, 8, stride=96), :]
                for j in range(24)
                for x in range(4)
            ]
            ordered = jnp.concatenate(rows, axis=0).astype(bf16)
            product = lax.dot_general(
                ordered, matrix_ref[s], (((0,), (0,)), ((), ())), preferred_element_type=f32
            )
            product = product.T * (1.0 / degree)
            if degree < 4:
                product = product.astype(bf16).astype(f32)
                term_ref[s] = product
                total_ref[s] = total_ref[s] + product
            else:
                out_ref[s] = (total_ref[s] + product).astype(bf16)


def propagate(blocks, current):
    share, orbitals, electrons = current.shape
    f32, bf16 = jnp.float32, jnp.bfloat16
    return pl.pallas_call(
        propagate_kernel,
        out_shape=jax.ShapeDtypeStruct(current.shape, bf16),
        scratch_shapes=[
            pltpu.VMEM((share, orbitals, orbitals), bf16),
            pltpu.VMEM((share, orbitals, electrons), f32),
            pltpu.VMEM((share, orbitals, electrons), f32),
        ],
        name="propagate",
    )(blocks, current)


def per_device(walkers, intersection_inverse, noise, half_cholesky, cholesky, comb_source):
    walk_local, row_count, electrons = walkers.shape
    vectors = cholesky.shape[2]
    z_count, x_count = lax.axis_size("z"), lax.axis_size("x")
    wide_count = z_count * x_count
    narrow_count = lax.axis_size(NARROW)
    plane_count = x_count * narrow_count
    share = walk_local // narrow_count
    rows_here = z_count * share
    z_at = lax.axis_index("z")
    wide_at = lax.axis_index(WIDE)
    narrow_at = lax.axis_index(NARROW)
    root_step = math.sqrt(time_step)
    f32, bf16, i32 = jnp.float32, jnp.bfloat16, jnp.int32

    with jax.named_scope("slots"):
        offset = comb_source - (wide_at - 1) * walk_local
        chosen = slot_walkers(walkers, offset, wide_count)
        chosen = chosen.reshape(narrow_count, share, row_count, electrons)
        chosen = exchange(chosen, NARROW)
        current = chosen.transpose(1, 0, 2, 3).reshape(share, narrow_count * row_count, electrons)

    with jax.named_scope("side"):
        own_noise = lax.dynamic_slice_in_dim(noise, narrow_at * share, share, 0)
        own_offset = lax.dynamic_slice_in_dim(offset, narrow_at * share, share, 0).astype(bf16)
        own_offset = jnp.broadcast_to(own_offset[:, None], (share, LANES))
        side = jnp.concatenate([own_noise, own_offset], axis=1)
        side = exchange(jnp.broadcast_to(side[None], (z_count,) + side.shape), ("z",))
        side = side.reshape(rows_here, vectors + LANES)

    with jax.named_scope("rotate"):
        rotated = jnp.einsum(
            "wiq,wqp->wpi", walkers, intersection_inverse, preferred_element_type=f32
        ).astype(bf16)
        rotated = rotated.reshape(walk_local, z_count, x_count, -1).transpose(2, 1, 0, 3)
        pairs = exchange(rotated.reshape(wide_count, walk_local, -1), WIDE_X)

    with jax.named_scope("bias"):
        pairs = pairs.reshape(x_count, z_count, narrow_count, share, -1).transpose(0, 2, 1, 3, 4)
        pairs = pairs.reshape(wide_count * walk_local, -1)
        partial = jnp.dot(pairs, half_cholesky.reshape(-1, vectors), preferred_element_type=f32)
        partial = partial.astype(bf16).reshape(plane_count, rows_here, vectors)
        partial = exchange(partial, PLANE)
        partial = jnp.sum(partial.astype(f32), axis=0).astype(bf16)
        partial = exchange(jnp.broadcast_to(partial[None], (z_count,) + partial.shape), ("z",))
        bias = jnp.sum(partial.astype(f32), axis=0)
        force_bias = lax.dynamic_slice_in_dim(bias, z_at * share, share, 0)

    with jax.named_scope("field"):
        aux = root_step * side[:, :vectors].astype(f32) + time_step * bias
        aux = jnp.concatenate([aux.astype(bf16), side[:, vectors:]], axis=1)
        aux = exchange(jnp.broadcast_to(aux[None], (plane_count,) + aux.shape), PLANE)
        aux = aux.reshape(plane_count * rows_here, vectors + LANES)
        slot = jnp.arange(plane_count * rows_here, dtype=i32)
        slot_x = slot // (narrow_count * rows_here)
        slot_z = (slot // share) % z_count
        source = aux[:, vectors].astype(i32) + (slot_z * x_count + slot_x - 1) * walk_local
        block, inner = source // walk_local, source % walk_local
        row = (block % x_count) * narrow_count + inner // share
        row = row * rows_here + (block // x_count) * share + inner % share
        pick = (row[:, None] == slot[None]).astype(bf16)
        fields = jnp.dot(pick, aux[:, :vectors], preferred_element_type=f32).astype(bf16)

    with jax.named_scope("operator"):
        operator = lax.dot_general(
            fields,
            packed_cholesky(cholesky),
            (((1,), (1,)), ((), ())),
            preferred_element_type=f32,
        ).astype(bf16)
        operator = exchange(operator.reshape(wide_count * narrow_count, share, -1), MIXED)

    with jax.named_scope("taylor"):
        propagated = propagate(operator.transpose(1, 0, 2), current)
        propagated = propagated.reshape(share, narrow_count, row_count, electrons)
        new_walkers = exchange(propagated.transpose(1, 0, 2, 3), NARROW)
    return (new_walkers.reshape(walk_local, row_count, electrons), force_bias)


def solution(mesh):
    fine = Mesh(mesh.devices.reshape(8, 4, 4, 2), ALL)
    in_specs = (
        P(WIDE, NARROW, None),
        P(WIDE, None, None),
        P(WIDE, None),
        P(WIDE, NARROW, None),
        P(NARROW, WIDE, None),
        P(WIDE),
    )
    out_specs = (P(WIDE, NARROW, None), P(ALL, None))
    return jax.shard_map(
        per_device, mesh=fine, in_specs=in_specs, out_specs=out_specs, check_vma=False
    )
```

```python
import math

import jax
import jax.numpy as jnp
from jax import lax
from jax.experimental import pallas as pl
from jax.experimental.pallas import tpu as pltpu
from jax.sharding import Mesh, PartitionSpec as P


time_step = 0.01
WIDE = ("z", "x")
WIDE_X = ("x", "z")
NARROW = ("y", "c")
PLANE = ("x", "y", "c")
MIXED = ("x", "y", "c", "z")
ALL = WIDE + NARROW
LANES = 128


def exchange(blocks, axes):
    return lax.all_to_all(blocks, axes, split_axis=0, concat_axis=0, tiled=True)


def ordered_kernel(at_ref, *refs):
    *piece_refs, out_ref = refs
    for k, piece_ref in enumerate(piece_refs):
        out_ref[at_ref[0] ^ k] = piece_ref[...]


def gathered(array, axis):
    count = lax.axis_size(axis)
    pieces = [array]
    for k in range(1, count):
        pieces.append(lax.ppermute(array, axis, [(i, i ^ k) for i in range(count)]))
    in_vmem = pl.BlockSpec(memory_space=pltpu.VMEM)
    return pl.pallas_call(
        ordered_kernel,
        in_specs=[pl.BlockSpec(memory_space=pltpu.SMEM)] + [in_vmem] * count,
        out_specs=in_vmem,
        out_shape=jax.ShapeDtypeStruct((count,) + array.shape, array.dtype),
        name="ordered",
    )(lax.axis_index(axis).astype(jnp.int32).reshape(1), *pieces)


def dealt(blocks, axes):
    count = lax.axis_size(axes)
    at = lax.axis_index(axes)
    pieces = []
    for k in range(count):
        piece = lax.dynamic_index_in_dim(blocks, at ^ k, 0, keepdims=False)
        if k:
            piece = lax.ppermute(piece, axes, [(i, i ^ k) for i in range(count)])
        pieces.append(piece)
    return pieces


def slot_walkers(walkers, offset, wide_count):
    up = [(i, (i + 1) % wide_count) for i in range(wide_count - 1)]
    down = [(j, i) for i, j in up]
    before = lax.ppermute(walkers, WIDE, up)
    after = lax.ppermute(walkers, WIDE, down)
    padded = jnp.concatenate([before, walkers, after], axis=0)
    return jnp.take(padded, offset, axis=0)


def packed_cholesky(cholesky):
    row_count, col_count, vectors = cholesky.shape
    by_col = cholesky.transpose(1, 0, 2)
    full = col_count * row_count // LANES
    rest = LANES - row_count
    tail = by_col[full:].reshape(full, rest, vectors)
    return jnp.concatenate([by_col[:full], tail], axis=1).reshape(full * LANES, vectors)


def propagate_kernel(at_ref, blocks_ref, *refs):
    *current_refs, out_ref, matrix_ref, term_ref, total_ref = refs
    share = blocks_ref.shape[0]
    f32, bf16 = jnp.float32, jnp.bfloat16
    lane = lax.broadcasted_iota(jnp.int32, (32, 128), 1)

    def assemble(s, carry):
        def rows_of(t, n):
            at = t * 128
            pieces = [
                blocks_ref[s, x * 64 + n * 8 : x * 64 + n * 8 + 8, at : at + 128]
                for x in range(4)
            ]
            return jnp.concatenate([piece.astype(f32) for piece in pieces], axis=0)

        for j in range(24):
            chunks = []
            for n in range(8):
                if j < 18:
                    chunk = rows_of(j, n)
                else:
                    q = 3 * (j - 18)
                    chunk = jnp.where(
                        lane < 32,
                        pltpu.roll(rows_of(q, n), 32, 1),
                        jnp.where(
                            lane < 64,
                            pltpu.roll(rows_of(q + 1, n), 64, 1),
                            pltpu.roll(rows_of(q + 2, n), 96, 1),
                        ),
                    )
                chunks.append(chunk)
            for half in range(2):
                first, second, third, fourth = chunks[4 * half : 4 * half + 4]
                second = pltpu.roll(second, 96, 1)
                third = pltpu.roll(third, 64, 1)
                fourth = pltpu.roll(fourth, 32, 1)
                tiles = (
                    jnp.where(lane < 96, first, second),
                    jnp.where(lane < 64, second, third),
                    jnp.where(lane < 32, third, fourth),
                )
                for k, tile in enumerate(tiles):
                    at = half * 384 + k * 128
                    matrix_ref[s, j * 32 : (j + 1) * 32, at : at + 128] = tile.astype(bf16)
        return carry

    lax.fori_loop(0, share, assemble, 0)
    narrow, _, rows_each, _ = out_ref.shape
    for k, current_ref in enumerate(current_refs):
        first_row = pl.multiple_of((at_ref[0] ^ k) * rows_each, 8)
        for s in range(share):
            start = current_ref[s].astype(f32)
            term_ref[s, pl.ds(first_row, rows_each), :] = start
            total_ref[s, pl.ds(first_row, rows_each), :] = start
    for degree in range(1, 5):
        for s in range(share):
            rows = [
                term_ref[s, pl.ds(x * 24 + j, 8, stride=96), :]
                for j in range(24)
                for x in range(4)
            ]
            ordered = jnp.concatenate(rows, axis=0).astype(bf16)
            product = lax.dot_general(
                ordered, matrix_ref[s], (((0,), (0,)), ((), ())), preferred_element_type=f32
            )
            product = product.T * (1.0 / degree)
            if degree < 4:
                product = product.astype(bf16).astype(f32)
                term_ref[s] = product
                total_ref[s] = total_ref[s] + product
            else:
                product = (total_ref[s] + product).astype(bf16)
                for n in range(narrow):
                    out_ref[n, s] = product[n * rows_each : (n + 1) * rows_each]


def propagate(narrow_at, blocks, current):
    narrow = len(current)
    share, rows_each, electrons = current[0].shape
    orbitals = narrow * rows_each
    f32, bf16 = jnp.float32, jnp.bfloat16
    in_vmem = pl.BlockSpec(memory_space=pltpu.VMEM)
    return pl.pallas_call(
        propagate_kernel,
        in_specs=[pl.BlockSpec(memory_space=pltpu.SMEM)] + [in_vmem] * (1 + narrow),
        out_specs=in_vmem,
        out_shape=jax.ShapeDtypeStruct((narrow, share, rows_each, electrons), bf16),
        scratch_shapes=[
            pltpu.VMEM((share, orbitals, orbitals), bf16),
            pltpu.VMEM((share, orbitals, electrons), f32),
            pltpu.VMEM((share, orbitals, electrons), f32),
        ],
        name="propagate",
    )(narrow_at.astype(jnp.int32).reshape(1), blocks, *current)


def per_device(walkers, intersection_inverse, noise, half_cholesky, cholesky, comb_source):
    walk_local, row_count, electrons = walkers.shape
    vectors = cholesky.shape[2]
    z_count, x_count = lax.axis_size("z"), lax.axis_size("x")
    wide_count = z_count * x_count
    narrow_count = lax.axis_size(NARROW)
    plane_count = x_count * narrow_count
    share = walk_local // narrow_count
    rows_here = z_count * share
    z_at = lax.axis_index("z")
    wide_at = lax.axis_index(WIDE)
    narrow_at = lax.axis_index(NARROW)
    root_step = math.sqrt(time_step)
    f32, bf16, i32 = jnp.float32, jnp.bfloat16, jnp.int32

    packed = packed_cholesky(cholesky)

    offset = comb_source - (wide_at - 1) * walk_local
    chosen = slot_walkers(walkers, offset, wide_count)

    chosen = chosen.reshape(narrow_count, share, row_count, electrons)
    current = dealt(chosen, NARROW)

    own_noise = lax.dynamic_slice_in_dim(noise, narrow_at * share, share, 0)
    own_offset = lax.dynamic_slice_in_dim(offset, narrow_at * share, share, 0).astype(bf16)
    own_offset = jnp.broadcast_to(own_offset[:, None], (share, LANES))
    side = jnp.concatenate([own_noise, own_offset], axis=1)
    side = gathered(side, "z").reshape(rows_here, vectors + LANES)

    rotated = jnp.einsum(
        "wiq,wqp->wpi", walkers, intersection_inverse, preferred_element_type=f32
    ).astype(bf16)
    rotated = rotated.reshape(walk_local, z_count, x_count, -1).transpose(2, 1, 0, 3)
    pairs = exchange(rotated.reshape(wide_count, walk_local, -1), WIDE_X)

    pairs = pairs.reshape(x_count, z_count, narrow_count, share, -1).transpose(0, 2, 1, 3, 4)
    pairs = pairs.reshape(wide_count * walk_local, -1)
    partial = jnp.dot(pairs, half_cholesky.reshape(-1, vectors), preferred_element_type=f32)
    partial = partial.astype(bf16).reshape(plane_count, rows_here, vectors)
    partial = exchange(partial, PLANE)

    partial = jnp.sum(partial.astype(f32), axis=0).astype(bf16)
    partial = exchange(jnp.broadcast_to(partial[None], (z_count,) + partial.shape), ("z",))
    bias = jnp.sum(partial.astype(f32), axis=0)
    force_bias = lax.dynamic_slice_in_dim(bias, z_at * share, share, 0)

    aux = root_step * side[:, :vectors].astype(f32) + time_step * bias
    aux = jnp.concatenate([aux.astype(bf16), side[:, vectors:]], axis=1)
    aux = exchange(jnp.broadcast_to(aux[None], (plane_count,) + aux.shape), PLANE)
    aux = aux.reshape(plane_count * rows_here, vectors + LANES)
    slot = jnp.arange(plane_count * rows_here, dtype=i32)
    slot_x = slot // (narrow_count * rows_here)
    slot_z = (slot // share) % z_count
    source = aux[:, vectors].astype(i32) + (slot_z * x_count + slot_x - 1) * walk_local
    block, inner = source // walk_local, source % walk_local
    row = (block % x_count) * narrow_count + inner // share
    row = row * rows_here + (block // x_count) * share + inner % share
    pick = (row[:, None] == slot[None]).astype(bf16)
    fields = jnp.dot(pick, aux[:, :vectors], preferred_element_type=f32).astype(bf16)

    operator = lax.dot_general(
        fields,
        packed,
        (((1,), (1,)), ((), ())),
        preferred_element_type=f32,
    ).astype(bf16)
    operator = exchange(operator.reshape(wide_count * narrow_count, share, -1), MIXED)

    propagated = propagate(narrow_at, operator.transpose(1, 0, 2), current)
    new_walkers = exchange(propagated, NARROW)
    return (new_walkers.reshape(walk_local, row_count, electrons), force_bias)


def solution(mesh):
    fine = Mesh(mesh.devices.reshape(8, 4, 4, 2), ALL)
    in_specs = (
        P(WIDE, NARROW, None),
        P(WIDE, None, None),
        P(WIDE, None),
        P(WIDE, NARROW, None),
        P(NARROW, WIDE, None),
        P(WIDE),
    )
    out_specs = (P(WIDE, NARROW, None), P(ALL, None))

    return jax.shard_map(
        per_device, mesh=fine, in_specs=in_specs, out_specs=out_specs, check_vma=False
    )
```

```python
import math

import jax
import jax.numpy as jnp
from jax import lax
from jax.experimental import pallas as pl
from jax.experimental.pallas import tpu as pltpu
from jax.sharding import Mesh, PartitionSpec as P


time_step = 0.01
WIDE = ("z", "x")
NARROW = ("y", "c")
PLANE = ("x", "y")
MIXED = ("c", "x", "y", "z")
ALL = WIDE + NARROW
LANES = 128


def exchange(blocks, axes):
    return lax.all_to_all(blocks, axes, split_axis=0, concat_axis=0, tiled=True)


def ordered_kernel(at_ref, pieces_ref, out_ref):
    for k in range(out_ref.shape[0]):
        out_ref[at_ref[0] ^ k] = pieces_ref[k]


def gathered(array, axis):
    count = lax.axis_size(axis)
    pieces = array[None]
    while pieces.shape[0] < count:
        bit = pieces.shape[0]
        received = lax.ppermute(pieces, axis, [(i, i ^ bit) for i in range(count)])
        pieces = jnp.concatenate([pieces, received], axis=0)
    in_vmem = pl.BlockSpec(memory_space=pltpu.VMEM)
    return pl.pallas_call(
        ordered_kernel,
        in_specs=[pl.BlockSpec(memory_space=pltpu.SMEM), in_vmem],
        out_specs=in_vmem,
        out_shape=jax.ShapeDtypeStruct(pieces.shape, array.dtype),
        name="ordered",
    )(lax.axis_index(axis).astype(jnp.int32).reshape(1), pieces)


def operator_kernel(at_ref, own_ref, other_ref, packed_ref, out_ref, fields_ref):
    f32, bf16, i32 = jnp.float32, jnp.bfloat16, jnp.int32
    vectors = packed_ref.shape[1]
    rows = own_ref.shape[0]
    core_at = at_ref[0]

    @pl.when(pl.program_id(0) == 0)
    def _():
        slot = lax.broadcasted_iota(i32, (rows, LANES), 0)
        lane = lax.broadcasted_iota(i32, (rows, LANES), 1)
        base = (((slot >> 1) & 7) * 4 + (slot >> 6) - 1) * 16
        tables = (own_ref, other_ref)
        for k, table in enumerate(tables):
            source = table[:, vectors:].astype(f32).astype(i32) + base
            block, inner = source >> 4, source & 15
            row = (((inner >> 1) & 1) ^ core_at) * rows + (block & 3) * 64
            row = row + (inner >> 2) * 16 + (block >> 2) * 2 + (inner & 1)
            fields = jnp.zeros((rows, vectors), f32)
            for half, picked in enumerate(tables):
                hits = [
                    (row == lane + (half * rows + at)).astype(f32).astype(bf16)
                    for at in range(0, rows, LANES)
                ]
                pick = jnp.concatenate(hits, axis=1)
                fields = fields + jnp.dot(
                    pick, picked[:, :vectors], preferred_element_type=f32
                )
            fields_ref[k ^ core_at] = fields.astype(bf16)

    for half in range(2):
        product = lax.dot_general(
            fields_ref[half], packed_ref[...], (((1,), (1,)), ((), ())), preferred_element_type=f32
        )
        out_ref[half * rows : (half + 1) * rows, :] = product.astype(bf16)


def operator_rows(core_at, own, other, packed):
    rows = own.shape[0]
    columns, vectors = packed.shape
    width = 384
    whole = pl.BlockSpec(own.shape, lambda i: (0, 0))
    return pl.pallas_call(
        operator_kernel,
        grid=(columns // width,),
        in_specs=[
            pl.BlockSpec(memory_space=pltpu.SMEM),
            whole,
            whole,
            pl.BlockSpec((width, vectors), lambda i: (i, 0)),
        ],
        out_specs=pl.BlockSpec((2 * rows, width), lambda i: (0, i)),
        out_shape=jax.ShapeDtypeStruct((2 * rows, columns), jnp.bfloat16),
        scratch_shapes=[pltpu.VMEM((2, rows, vectors), jnp.bfloat16)],
        name="operator_rows",
    )(core_at.astype(jnp.int32).reshape(1), own, other, packed)


def dealt(blocks, axes):
    count = lax.axis_size(axes)
    at = lax.axis_index(axes)
    pieces = []
    for k in range(count):
        piece = lax.dynamic_index_in_dim(blocks, at ^ k, 0, keepdims=False)
        if k:
            piece = lax.ppermute(piece, axes, [(i, i ^ k) for i in range(count)])
        pieces.append(piece)
    return pieces


def slot_walkers(walkers, offset, wide_count):
    up = [(i, (i + 1) % wide_count) for i in range(wide_count - 1)]
    down = [(j, i) for i, j in up]
    before = lax.ppermute(walkers, WIDE, up)
    after = lax.ppermute(walkers, WIDE, down)
    padded = jnp.concatenate([before, walkers, after], axis=0)
    return jnp.take(padded, offset, axis=0)


def packed_cholesky(cholesky):
    row_count, col_count, vectors = cholesky.shape
    by_col = cholesky.transpose(1, 0, 2)
    full = col_count * row_count // LANES
    rest = LANES - row_count
    tail = by_col[full:].reshape(full, rest, vectors)
    return jnp.concatenate([by_col[:full], tail], axis=1).reshape(full * LANES, vectors)


def propagate_kernel(at_ref, blocks_ref, *refs):
    *current_refs, out_ref, matrix_ref, term_ref, total_ref = refs
    share = blocks_ref.shape[0]
    f32, bf16 = jnp.float32, jnp.bfloat16
    lane = lax.broadcasted_iota(jnp.int32, (32, 128), 1)

    def assemble(s, carry):
        def rows_of(t, n):
            at = t * 128
            first = (n & 1) * 128 + (n >> 1) * 8
            pieces = [
                blocks_ref[s, first + x * 32 : first + x * 32 + 8, at : at + 128]
                for x in range(4)
            ]
            return jnp.concatenate([piece.astype(f32) for piece in pieces], axis=0)

        for j in range(24):
            chunks = []
            for n in range(8):
                if j < 18:
                    chunk = rows_of(j, n)
                else:
                    q = 3 * (j - 18)
                    chunk = jnp.where(
                        lane < 32,
                        pltpu.roll(rows_of(q, n), 32, 1),
                        jnp.where(
                            lane < 64,
                            pltpu.roll(rows_of(q + 1, n), 64, 1),
                            pltpu.roll(rows_of(q + 2, n), 96, 1),
                        ),
                    )
                chunks.append(chunk)
            for half in range(2):
                first, second, third, fourth = chunks[4 * half : 4 * half + 4]
                second = pltpu.roll(second, 96, 1)
                third = pltpu.roll(third, 64, 1)
                fourth = pltpu.roll(fourth, 32, 1)
                tiles = (
                    jnp.where(lane < 96, first, second),
                    jnp.where(lane < 64, second, third),
                    jnp.where(lane < 32, third, fourth),
                )
                for k, tile in enumerate(tiles):
                    at = half * 384 + k * 128
                    matrix_ref[s, j * 32 : (j + 1) * 32, at : at + 128] = tile.astype(bf16)
        return carry

    lax.fori_loop(0, share, assemble, 0)
    narrow, _, rows_each, _ = out_ref.shape
    for k, current_ref in enumerate(current_refs):
        first_row = pl.multiple_of((at_ref[0] ^ k) * rows_each, 8)
        for s in range(share):
            start = current_ref[s].astype(f32)
            term_ref[s, pl.ds(first_row, rows_each), :] = start
            total_ref[s, pl.ds(first_row, rows_each), :] = start
    for degree in range(1, 5):
        for s in range(share):
            rows = [
                term_ref[s, pl.ds(x * 24 + j, 8, stride=96), :]
                for j in range(24)
                for x in range(4)
            ]
            ordered = jnp.concatenate(rows, axis=0).astype(bf16)
            product = lax.dot_general(
                ordered, matrix_ref[s], (((0,), (0,)), ((), ())), preferred_element_type=f32
            )
            product = product.T * (1.0 / degree)
            if degree < 4:
                product = product.astype(bf16).astype(f32)
                term_ref[s] = product
                total_ref[s] = total_ref[s] + product
            else:
                product = (total_ref[s] + product).astype(bf16)
                for n in range(narrow):
                    out_ref[n, s] = product[n * rows_each : (n + 1) * rows_each]


def propagate(narrow_at, blocks, current):
    narrow = len(current)
    share, rows_each, electrons = current[0].shape
    orbitals = narrow * rows_each
    f32, bf16 = jnp.float32, jnp.bfloat16
    in_vmem = pl.BlockSpec(memory_space=pltpu.VMEM)
    return pl.pallas_call(
        propagate_kernel,
        in_specs=[pl.BlockSpec(memory_space=pltpu.SMEM)] + [in_vmem] * (1 + narrow),
        out_specs=in_vmem,
        out_shape=jax.ShapeDtypeStruct((narrow, share, rows_each, electrons), bf16),
        scratch_shapes=[
            pltpu.VMEM((share, orbitals, orbitals), bf16),
            pltpu.VMEM((share, orbitals, electrons), f32),
            pltpu.VMEM((share, orbitals, electrons), f32),
        ],
        name="propagate",
    )(narrow_at.astype(jnp.int32).reshape(1), blocks, *current)


def per_device(walkers, intersection_inverse, noise, half_cholesky, cholesky, comb_source):
    walk_local, row_count, electrons = walkers.shape
    vectors = cholesky.shape[2]
    z_count, x_count = lax.axis_size("z"), lax.axis_size("x")
    wide_count = z_count * x_count
    narrow_count = lax.axis_size(NARROW)
    plane_count = lax.axis_size(PLANE)
    core_at = lax.axis_index("c")
    swap = [(0, 1), (1, 0)]
    share = walk_local // narrow_count
    rows_here = z_count * share
    z_at = lax.axis_index("z")
    wide_at = lax.axis_index(WIDE)
    narrow_at = lax.axis_index(NARROW)
    root_step = math.sqrt(time_step)
    f32, bf16 = jnp.float32, jnp.bfloat16

    packed = packed_cholesky(cholesky)

    offset = comb_source - (wide_at - 1) * walk_local
    chosen = slot_walkers(walkers, offset, wide_count)

    chosen = chosen.reshape(narrow_count, share, row_count, electrons)
    current = dealt(chosen, NARROW)

    own_noise = lax.dynamic_slice_in_dim(noise, narrow_at * share, share, 0)
    own_offset = lax.dynamic_slice_in_dim(offset, narrow_at * share, share, 0).astype(bf16)
    own_offset = jnp.broadcast_to(own_offset[:, None], (share, LANES))
    side = jnp.concatenate([own_noise, own_offset], axis=1)
    side = gathered(side, "z").reshape(rows_here, vectors + LANES)

    rotated = jnp.einsum(
        "wiq,wqp->wpi", walkers, intersection_inverse, preferred_element_type=f32
    ).astype(bf16)
    rotated = rotated.reshape(walk_local, wide_count, -1).transpose(1, 0, 2)
    pairs = exchange(rotated, WIDE)

    y_count, core_count = lax.axis_size("y"), lax.axis_size("c")
    pairs = pairs.reshape(z_count, x_count, y_count, core_count, share, -1)
    pairs = pairs.transpose(3, 1, 2, 0, 4, 5).reshape(core_count, plane_count * rows_here, -1)
    half_flat = half_cholesky.reshape(-1, vectors)
    mine = lax.dynamic_index_in_dim(pairs, core_at, 0, keepdims=False)
    theirs = lax.dynamic_index_in_dim(pairs, 1 - core_at, 0, keepdims=False)
    sent = jnp.dot(theirs, half_flat, preferred_element_type=f32).astype(bf16)
    received = lax.ppermute(sent, "c", swap)
    partial = jnp.dot(mine, half_flat, preferred_element_type=f32) + received.astype(f32)
    partial = partial.astype(bf16).reshape(plane_count, rows_here, vectors)
    partial = exchange(partial, PLANE)

    partial = jnp.sum(partial.astype(f32), axis=0).astype(bf16)
    partial = exchange(jnp.broadcast_to(partial[None], (z_count,) + partial.shape), ("z",))
    bias = jnp.sum(partial.astype(f32), axis=0)
    force_bias = lax.dynamic_slice_in_dim(bias, z_at * share, share, 0)

    aux = root_step * side[:, :vectors].astype(f32) + time_step * bias
    aux = jnp.concatenate([aux.astype(bf16), side[:, vectors:]], axis=1)
    aux = exchange(jnp.broadcast_to(aux[None], (plane_count,) + aux.shape), PLANE)
    aux = aux.reshape(plane_count * rows_here, vectors + LANES)
    other = lax.ppermute(aux, "c", swap)

    operator = operator_rows(core_at, aux, other, packed)
    operator = exchange(operator.reshape(wide_count * narrow_count, share, -1), MIXED)

    propagated = propagate(narrow_at, operator.transpose(1, 0, 2), current)
    new_walkers = exchange(propagated, NARROW)
    return (new_walkers.reshape(walk_local, row_count, electrons), force_bias)


def solution(mesh):
    fine = Mesh(mesh.devices.reshape(8, 4, 4, 2), ALL)
    in_specs = (
        P(WIDE, NARROW, None),
        P(WIDE, None, None),
        P(WIDE, None),
        P(WIDE, NARROW, None),
        P(NARROW, WIDE, None),
        P(WIDE),
    )
    out_specs = (P(WIDE, NARROW, None), P(ALL, None))

    return jax.shard_map(
        per_device, mesh=fine, in_specs=in_specs, out_specs=out_specs, check_vma=False
    )
```

```python
import math

import jax
import jax.numpy as jnp
from jax import lax
from jax.experimental import pallas as pl
from jax.experimental.pallas import tpu as pltpu
from jax.sharding import Mesh, PartitionSpec as P


time_step = 0.01
WIDE = ("z", "x")
NARROW = ("y", "c")
PLANE = ("x", "y")
MIXED = ("c", "x", "y", "z")
ALL = WIDE + NARROW
LANES = 128


def exchange(blocks, axes):
    return lax.all_to_all(blocks, axes, split_axis=0, concat_axis=0, tiled=True)


def fields_kernel(at_ref, own_hbm, other_hbm, out_ref, own_ref, other_ref, sems):
    f32, bf16, i32 = jnp.float32, jnp.bfloat16, jnp.int32
    vectors = out_ref.shape[2]
    rows = own_ref.shape[0]
    core_at = at_ref[0]
    own_copy = pltpu.make_async_copy(own_hbm, own_ref, sems.at[0])
    other_copy = pltpu.make_async_copy(other_hbm, other_ref, sems.at[1])
    own_copy.start()
    other_copy.start()
    own_copy.wait()
    other_copy.wait()
    slot = lax.broadcasted_iota(i32, (rows, LANES), 0)
    lane = lax.broadcasted_iota(i32, (rows, LANES), 1)
    base = (((slot >> 1) & 7) * 4 + (slot >> 6) - 1) * 16
    tables = (own_ref, other_ref)
    for k, table in enumerate(tables):
        source = table[:, vectors:].astype(f32).astype(i32) + base
        block, inner = source >> 4, source & 15
        row = (((inner >> 1) & 1) ^ core_at) * rows + (block & 3) * 64
        row = row + (inner >> 2) * 16 + (block >> 2) * 2 + (inner & 1)
        fields = jnp.zeros((rows, vectors), f32)
        for half, picked in enumerate(tables):
            hits = [
                (row == lane + (half * rows + at)).astype(f32).astype(bf16)
                for at in range(0, rows, LANES)
            ]
            pick = jnp.concatenate(hits, axis=1)
            fields = fields + jnp.dot(pick, picked[:, :vectors], preferred_element_type=f32)
        out_ref[k ^ core_at] = fields.astype(bf16)


def picked_fields(core_at, own, other):
    rows, width = own.shape
    vectors = width - LANES
    anywhere = pl.BlockSpec(memory_space=pl.ANY)
    fields = pl.pallas_call(
        fields_kernel,
        in_specs=[pl.BlockSpec(memory_space=pltpu.SMEM), anywhere, anywhere],
        out_specs=pl.BlockSpec(memory_space=pltpu.VMEM),
        out_shape=jax.ShapeDtypeStruct((2, rows, vectors), own.dtype),
        scratch_shapes=[
            pltpu.VMEM(own.shape, own.dtype),
            pltpu.VMEM(own.shape, own.dtype),
            pltpu.SemaphoreType.DMA((2,)),
        ],
        name="fields",
    )(core_at.astype(jnp.int32).reshape(1), own, other)
    return fields.reshape(2 * rows, vectors)


def dealt(blocks, axes):
    count = lax.axis_size(axes)
    at = lax.axis_index(axes)
    pieces = []
    for k in range(count):
        piece = lax.dynamic_index_in_dim(blocks, at ^ k, 0, keepdims=False)
        if k:
            piece = lax.ppermute(piece, axes, [(i, i ^ k) for i in range(count)])
        pieces.append(piece)
    return pieces


def slot_walkers(walkers, offset, wide_count):
    up = [(i, (i + 1) % wide_count) for i in range(wide_count - 1)]
    down = [(j, i) for i, j in up]
    before = lax.ppermute(walkers, WIDE, up)
    after = lax.ppermute(walkers, WIDE, down)
    padded = jnp.concatenate([before, walkers, after], axis=0)
    return jnp.take(padded, offset, axis=0)


def pack_kernel(chol_ref, out_ref, wide_ref):
    row_count, col_count, width = chol_ref.shape
    f32, bf16 = jnp.float32, jnp.bfloat16
    full = out_ref.shape[0]
    for at in range(0, width, LANES):
        wide_ref[...] = chol_ref[:, :, at : at + LANES].astype(f32).reshape(row_count * col_count, LANES)
        for j in range(full):
            out_ref[j, :row_count, at : at + LANES] = wide_ref[pl.ds(j, row_count, stride=col_count), :].astype(bf16)
        for j in range(full, col_count):
            column = wide_ref[pl.ds(j, row_count, stride=col_count), :].astype(bf16)
            for p in range(3):
                out_ref[3 * (j - full) + p, row_count:, at : at + LANES] = column[p * 32 : (p + 1) * 32]


def packed_cholesky(cholesky):
    row_count, col_count, vectors = cholesky.shape
    full = col_count * row_count // LANES
    width = 256
    packed = pl.pallas_call(
        pack_kernel,
        grid=(vectors // width,),
        in_specs=[pl.BlockSpec((row_count, col_count, width), lambda i: (0, 0, i))],
        out_specs=pl.BlockSpec((full, LANES, width), lambda i: (0, 0, i)),
        out_shape=jax.ShapeDtypeStruct((full, LANES, vectors), cholesky.dtype),
        scratch_shapes=[pltpu.VMEM((row_count * col_count, LANES), jnp.float32)],
        name="pack",
    )(cholesky)
    return packed.reshape(full * LANES, vectors)


def propagate_kernel(at_ref, blocks_ref, *refs):
    *current_refs, out_ref, matrix_ref, term_ref, total_ref = refs
    share = blocks_ref.shape[0]
    f32, bf16 = jnp.float32, jnp.bfloat16
    lane = lax.broadcasted_iota(jnp.int32, (32, 128), 1)

    def assemble(s, carry):
        def rows_of(t, n):
            at = t * 128
            first = (n & 1) * 128 + (n >> 1) * 8
            pieces = [
                blocks_ref[s, first + x * 32 : first + x * 32 + 8, at : at + 128]
                for x in range(4)
            ]
            return jnp.concatenate([piece.astype(f32) for piece in pieces], axis=0)

        for j in range(24):
            chunks = []
            for n in range(8):
                if j < 18:
                    chunk = rows_of(j, n)
                else:
                    q = 3 * (j - 18)
                    chunk = jnp.where(
                        lane < 32,
                        pltpu.roll(rows_of(q, n), 32, 1),
                        jnp.where(
                            lane < 64,
                            pltpu.roll(rows_of(q + 1, n), 64, 1),
                            pltpu.roll(rows_of(q + 2, n), 96, 1),
                        ),
                    )
                chunks.append(chunk)
            for half in range(2):
                first, second, third, fourth = chunks[4 * half : 4 * half + 4]
                second = pltpu.roll(second, 96, 1)
                third = pltpu.roll(third, 64, 1)
                fourth = pltpu.roll(fourth, 32, 1)
                tiles = (
                    jnp.where(lane < 96, first, second),
                    jnp.where(lane < 64, second, third),
                    jnp.where(lane < 32, third, fourth),
                )
                for k, tile in enumerate(tiles):
                    at = half * 384 + k * 128
                    matrix_ref[s, j * 32 : (j + 1) * 32, at : at + 128] = tile.astype(bf16)
        return carry

    lax.fori_loop(0, share, assemble, 0)
    narrow, _, rows_each, _ = out_ref.shape
    for k, current_ref in enumerate(current_refs):
        first_row = pl.multiple_of((at_ref[0] ^ k) * rows_each, 8)
        for s in range(share):
            start = current_ref[s].astype(f32)
            term_ref[s, pl.ds(first_row, rows_each), :] = start
            total_ref[s, pl.ds(first_row, rows_each), :] = start
    for degree in range(1, 5):
        for s in range(share):
            rows = [
                term_ref[s, pl.ds(x * 24 + j, 8, stride=96), :]
                for j in range(24)
                for x in range(4)
            ]
            ordered = jnp.concatenate(rows, axis=0).astype(bf16)
            product = lax.dot_general(
                ordered, matrix_ref[s], (((0,), (0,)), ((), ())), preferred_element_type=f32
            )
            product = product.T * (1.0 / degree)
            if degree < 4:
                product = product.astype(bf16).astype(f32)
                term_ref[s] = product
                total_ref[s] = total_ref[s] + product
            else:
                product = (total_ref[s] + product).astype(bf16)
                for n in range(narrow):
                    out_ref[n, s] = product[n * rows_each : (n + 1) * rows_each]


def propagate(narrow_at, blocks, current):
    narrow = len(current)
    share, rows_each, electrons = current[0].shape
    orbitals = narrow * rows_each
    f32, bf16 = jnp.float32, jnp.bfloat16
    in_vmem = pl.BlockSpec(memory_space=pltpu.VMEM)
    return pl.pallas_call(
        propagate_kernel,
        in_specs=[pl.BlockSpec(memory_space=pltpu.SMEM)] + [in_vmem] * (1 + narrow),
        out_specs=in_vmem,
        out_shape=jax.ShapeDtypeStruct((narrow, share, rows_each, electrons), bf16),
        scratch_shapes=[
            pltpu.VMEM((share, orbitals, orbitals), bf16),
            pltpu.VMEM((share, orbitals, electrons), f32),
            pltpu.VMEM((share, orbitals, electrons), f32),
        ],
        name="propagate",
    )(narrow_at.astype(jnp.int32).reshape(1), blocks, *current)


def per_device(walkers, intersection_inverse, noise, half_cholesky, cholesky, comb_source):
    walk_local, row_count, electrons = walkers.shape
    vectors = cholesky.shape[2]
    z_count, x_count = lax.axis_size("z"), lax.axis_size("x")
    wide_count = z_count * x_count
    narrow_count = lax.axis_size(NARROW)
    plane_count = lax.axis_size(PLANE)
    core_at = lax.axis_index("c")
    swap = [(0, 1), (1, 0)]
    share = walk_local // narrow_count
    rows_here = z_count * share
    z_at = lax.axis_index("z")
    wide_at = lax.axis_index(WIDE)
    narrow_at = lax.axis_index(NARROW)
    root_step = math.sqrt(time_step)
    f32, bf16 = jnp.float32, jnp.bfloat16

    packed = packed_cholesky(cholesky)

    offset = comb_source - (wide_at - 1) * walk_local
    chosen = slot_walkers(walkers, offset, wide_count)

    chosen = chosen.reshape(narrow_count, share, row_count, electrons)
    current = dealt(chosen, NARROW)

    own_noise = lax.dynamic_slice_in_dim(noise, narrow_at * share, share, 0)
    own_noise = own_noise.reshape(rows_here, LANES)
    own_offset = lax.dynamic_slice_in_dim(offset, narrow_at * share, share, 0).astype(bf16)
    own_offset = jnp.broadcast_to(own_offset[:, None, None], (share, z_count, LANES))
    side = jnp.concatenate([own_noise, own_offset.reshape(rows_here, LANES)], axis=1)

    rotated = jnp.einsum(
        "wiq,wqp->wpi", walkers, intersection_inverse, preferred_element_type=f32
    ).astype(bf16)
    rotated = rotated.reshape(walk_local, wide_count, -1).transpose(1, 0, 2)
    pairs = exchange(rotated, WIDE)

    y_count, core_count = lax.axis_size("y"), lax.axis_size("c")
    pairs = pairs.reshape(z_count, x_count, y_count, core_count, share, -1)
    pairs = pairs.transpose(3, 1, 2, 0, 4, 5).reshape(core_count, plane_count * rows_here, -1)
    half_flat = half_cholesky.reshape(-1, vectors)
    mine = lax.dynamic_index_in_dim(pairs, core_at, 0, keepdims=False)
    theirs = lax.dynamic_index_in_dim(pairs, 1 - core_at, 0, keepdims=False)
    sent = jnp.dot(theirs, half_flat, preferred_element_type=f32).astype(bf16)
    received = lax.ppermute(sent, "c", swap)
    partial = jnp.dot(mine, half_flat, preferred_element_type=f32) + received.astype(f32)
    partial = partial.astype(bf16).reshape(plane_count, rows_here, vectors)
    partial = exchange(partial, PLANE)

    partial = jnp.sum(partial.astype(f32), axis=0).astype(bf16)
    partial = jnp.concatenate([partial, side], axis=1)
    partial = exchange(jnp.broadcast_to(partial[None], (z_count,) + partial.shape), ("z",))
    bias = jnp.sum(partial[:, :, :vectors].astype(f32), axis=0)
    force_bias = lax.dynamic_slice_in_dim(bias, z_at * share, share, 0)

    noises = partial[:, :, vectors : vectors + LANES].reshape(rows_here, vectors)
    offsets = partial[:, ::z_count, vectors + LANES :].reshape(rows_here, LANES)
    aux = root_step * noises.astype(f32) + time_step * bias
    aux = jnp.concatenate([aux.astype(bf16), offsets], axis=1)
    aux = exchange(jnp.broadcast_to(aux[None], (plane_count,) + aux.shape), PLANE)
    aux = aux.reshape(plane_count * rows_here, vectors + LANES)
    other = lax.ppermute(aux, "c", swap)

    fields = picked_fields(core_at, aux, other)
    operator = lax.dot_general(
        fields, packed, (((1,), (1,)), ((), ())), preferred_element_type=f32
    ).astype(bf16)
    operator = exchange(operator.reshape(wide_count * narrow_count, share, -1), MIXED)

    propagated = propagate(narrow_at, operator.transpose(1, 0, 2), current)
    new_walkers = exchange(propagated, NARROW)
    return (new_walkers.reshape(walk_local, row_count, electrons), force_bias)


def solution(mesh):
    fine = Mesh(mesh.devices.reshape(8, 4, 4, 2), ALL)
    in_specs = (
        P(WIDE, NARROW, None),
        P(WIDE, None, None),
        P(WIDE, None),
        P(WIDE, NARROW, None),
        P(NARROW, WIDE, None),
        P(WIDE),
    )
    out_specs = (P(WIDE, NARROW, None), P(ALL, None))

    return jax.shard_map(
        per_device, mesh=fine, in_specs=in_specs, out_specs=out_specs, check_vma=False
    )
```

```python
import math

import jax
import jax.numpy as jnp
from jax import lax
from jax.experimental import pallas as pl
from jax.experimental.pallas import tpu as pltpu
from jax.sharding import Mesh, PartitionSpec as P


time_step = 0.01
WIDE = ("z", "x")
NARROW = ("y", "c")
PLANE = ("x", "y")
MIXED = ("c", "x", "y", "z")
ALL = WIDE + NARROW
LANES = 128


def exchange(blocks, axes):
    return lax.all_to_all(blocks, axes, split_axis=0, concat_axis=0, tiled=True)


def in_vmem(array):
    return pltpu.with_memory_space_constraint(array, pltpu.VMEM)


def in_hbm(array):
    return pltpu.with_memory_space_constraint(array, pltpu.HBM)


def operator_kernel(
    at_ref, own_ref, other_ref, packed_hbm, out_hbm, fields_ref, packed_ref, out_ref, in_sems, out_sems
):
    f32, bf16, i32 = jnp.float32, jnp.bfloat16, jnp.int32
    steps, width, vectors = packed_ref.shape
    rows = own_ref.shape[0]
    core_at = at_ref[0]
    fetches = [
        pltpu.make_async_copy(
            packed_hbm.at[pl.ds(i * width, width), :], packed_ref.at[i], in_sems.at[i]
        )
        for i in range(steps)
    ]
    for fetch in fetches:
        fetch.start()
    slot = lax.broadcasted_iota(i32, (rows, LANES), 0)
    lane = lax.broadcasted_iota(i32, (rows, LANES), 1)
    base = (((slot >> 1) & 7) * 4 + (slot >> 6) - 1) * 16
    tables = (own_ref, other_ref)
    for k, table in enumerate(tables):
        source = table[:, vectors:].astype(f32).astype(i32) + base
        block, inner = source >> 4, source & 15
        row = (((inner >> 1) & 1) ^ core_at) * rows + (block & 3) * 64
        row = row + (inner >> 2) * 16 + (block >> 2) * 2 + (inner & 1)
        fields = jnp.zeros((rows, vectors), f32)
        for half, picked in enumerate(tables):
            hits = [
                (row == lane + (half * rows + at)).astype(f32).astype(bf16)
                for at in range(0, rows, LANES)
            ]
            pick = jnp.concatenate(hits, axis=1)
            fields = fields + jnp.dot(pick, picked[:, :vectors], preferred_element_type=f32)
        fields_ref[k ^ core_at] = fields.astype(bf16)

    writes = []
    for i in range(steps):
        fetches[i].wait()
        for k in range(2):
            product = lax.dot_general(
                fields_ref[k], packed_ref[i], (((1,), (1,)), ((), ())), preferred_element_type=f32
            )
            product = product.astype(bf16).reshape(rows // 2, 2, width)
            out_ref[i, k * (rows // 2) : (k + 1) * (rows // 2)] = product
        write = pltpu.make_async_copy(
            out_ref.at[i], out_hbm.at[:, :, pl.ds(i * width, width)], out_sems.at[i]
        )
        write.start()
        writes.append(write)
    for write in writes:
        write.wait()


def operator_blocks(core_at, own, other, packed):
    rows, _ = own.shape
    columns, vectors = packed.shape
    steps = 3
    width = columns // steps
    whole = pl.BlockSpec(memory_space=pltpu.VMEM)
    anywhere = pl.BlockSpec(memory_space=pltpu.HBM)
    return pl.pallas_call(
        operator_kernel,
        in_specs=[pl.BlockSpec(memory_space=pltpu.SMEM), whole, whole, anywhere],
        out_specs=anywhere,
        out_shape=jax.ShapeDtypeStruct((rows, 2, columns), own.dtype),
        scratch_shapes=[
            pltpu.VMEM((2, rows, vectors), own.dtype),
            pltpu.VMEM((steps, width, vectors), own.dtype),
            pltpu.VMEM((steps, rows, 2, width), own.dtype),
            pltpu.SemaphoreType.DMA((steps,)),
            pltpu.SemaphoreType.DMA((steps,)),
        ],
        compiler_params=pltpu.CompilerParams(vmem_limit_bytes=28 * 2**20),
        name="operator_blocks",
    )(core_at.astype(jnp.int32).reshape(1), in_vmem(own), in_vmem(other), in_hbm(packed))


def dealt(blocks, axes):
    count = lax.axis_size(axes)
    at = lax.axis_index(axes)
    pieces = []
    for k in range(count):
        piece = lax.dynamic_index_in_dim(blocks, at ^ k, 0, keepdims=False)
        if k:
            piece = lax.ppermute(piece, axes, [(i, i ^ k) for i in range(count)])
        pieces.append(piece)
    return pieces


def slot_walkers(walkers, offset, wide_count):
    up = [(i, (i + 1) % wide_count) for i in range(wide_count - 1)]
    down = [(j, i) for i, j in up]
    before = lax.ppermute(walkers, WIDE, up)
    after = lax.ppermute(walkers, WIDE, down)
    padded = jnp.concatenate([before, walkers, after], axis=0)
    return jnp.take(padded, offset, axis=0)


def pack_kernel(chol_ref, out_ref, wide_ref):
    row_count, col_count, width = chol_ref.shape
    f32, bf16 = jnp.float32, jnp.bfloat16
    full = out_ref.shape[0]
    for at in range(0, width, LANES):
        wide_ref[...] = chol_ref[:, :, at : at + LANES].astype(f32).reshape(row_count * col_count, LANES)
        for j in range(full):
            out_ref[j, :row_count, at : at + LANES] = wide_ref[pl.ds(j, row_count, stride=col_count), :].astype(bf16)
        for j in range(full, col_count):
            column = wide_ref[pl.ds(j, row_count, stride=col_count), :].astype(bf16)
            for p in range(3):
                out_ref[3 * (j - full) + p, row_count:, at : at + LANES] = column[p * 32 : (p + 1) * 32]


def packed_cholesky(cholesky):
    row_count, col_count, vectors = cholesky.shape
    full = col_count * row_count // LANES
    width = 256
    packed = pl.pallas_call(
        pack_kernel,
        grid=(vectors // width,),
        in_specs=[pl.BlockSpec((row_count, col_count, width), lambda i: (0, 0, i))],
        out_specs=pl.BlockSpec((full, LANES, width), lambda i: (0, 0, i)),
        out_shape=jax.ShapeDtypeStruct((full, LANES, vectors), cholesky.dtype),
        scratch_shapes=[pltpu.VMEM((row_count * col_count, LANES), jnp.float32)],
        name="pack",
    )(cholesky)
    return packed.reshape(full * LANES, vectors)


def propagate_kernel(at_ref, blocks_ref, *refs):
    *current_refs, out_ref, matrix_ref, term_ref, total_ref = refs
    share = blocks_ref.shape[0]
    f32, bf16 = jnp.float32, jnp.bfloat16
    lane = lax.broadcasted_iota(jnp.int32, (32, 128), 1)

    def assemble(s, carry):
        def rows_of(t, n):
            at = t * 128
            first = (n & 1) * 128 + (n >> 1) * 8
            pieces = [
                blocks_ref[s, first + x * 32 : first + x * 32 + 8, at : at + 128]
                for x in range(4)
            ]
            return jnp.concatenate([piece.astype(f32) for piece in pieces], axis=0)

        for j in range(24):
            chunks = []
            for n in range(8):
                if j < 18:
                    chunk = rows_of(j, n)
                else:
                    q = 3 * (j - 18)
                    chunk = jnp.where(
                        lane < 32,
                        pltpu.roll(rows_of(q, n), 32, 1),
                        jnp.where(
                            lane < 64,
                            pltpu.roll(rows_of(q + 1, n), 64, 1),
                            pltpu.roll(rows_of(q + 2, n), 96, 1),
                        ),
                    )
                chunks.append(chunk)
            for half in range(2):
                first, second, third, fourth = chunks[4 * half : 4 * half + 4]
                second = pltpu.roll(second, 96, 1)
                third = pltpu.roll(third, 64, 1)
                fourth = pltpu.roll(fourth, 32, 1)
                tiles = (
                    jnp.where(lane < 96, first, second),
                    jnp.where(lane < 64, second, third),
                    jnp.where(lane < 32, third, fourth),
                )
                for k, tile in enumerate(tiles):
                    at = half * 384 + k * 128
                    matrix_ref[s, j * 32 : (j + 1) * 32, at : at + 128] = tile.astype(bf16)
        return carry

    lax.fori_loop(0, share, assemble, 0)
    narrow, _, rows_each, _ = out_ref.shape
    for k, current_ref in enumerate(current_refs):
        first_row = pl.multiple_of((at_ref[0] ^ k) * rows_each, 8)
        for s in range(share):
            start = current_ref[s].astype(f32)
            term_ref[s, pl.ds(first_row, rows_each), :] = start
            total_ref[s, pl.ds(first_row, rows_each), :] = start
    for degree in range(1, 5):
        for s in range(share):
            rows = [
                term_ref[s, pl.ds(x * 24 + j, 8, stride=96), :]
                for j in range(24)
                for x in range(4)
            ]
            ordered = jnp.concatenate(rows, axis=0).astype(bf16)
            product = lax.dot_general(
                ordered, matrix_ref[s], (((0,), (0,)), ((), ())), preferred_element_type=f32
            )
            product = product.T * (1.0 / degree)
            if degree < 4:
                product = product.astype(bf16).astype(f32)
                term_ref[s] = product
                total_ref[s] = total_ref[s] + product
            else:
                product = (total_ref[s] + product).astype(bf16)
                for n in range(narrow):
                    out_ref[n, s] = product[n * rows_each : (n + 1) * rows_each]


def propagate(narrow_at, blocks, current):
    narrow = len(current)
    share, rows_each, electrons = current[0].shape
    orbitals = narrow * rows_each
    f32, bf16 = jnp.float32, jnp.bfloat16
    whole = pl.BlockSpec(memory_space=pltpu.VMEM)
    return pl.pallas_call(
        propagate_kernel,
        in_specs=[pl.BlockSpec(memory_space=pltpu.SMEM)] + [whole] * (1 + narrow),
        out_specs=whole,
        out_shape=pltpu.VMEM((narrow, share, rows_each, electrons), bf16),
        scratch_shapes=[
            pltpu.VMEM((share, orbitals, orbitals), bf16),
            pltpu.VMEM((share, orbitals, electrons), f32),
            pltpu.VMEM((share, orbitals, electrons), f32),
        ],
        compiler_params=pltpu.CompilerParams(vmem_limit_bytes=24 * 2**20),
        name="propagate",
    )(narrow_at.astype(jnp.int32).reshape(1), in_vmem(blocks), *map(in_vmem, current))


def per_device(walkers, intersection_inverse, noise, half_cholesky, cholesky, comb_source):
    walk_local, row_count, electrons = walkers.shape
    vectors = cholesky.shape[2]
    z_count, x_count = lax.axis_size("z"), lax.axis_size("x")
    wide_count = z_count * x_count
    narrow_count = lax.axis_size(NARROW)
    plane_count = lax.axis_size(PLANE)
    core_at = lax.axis_index("c")
    swap = [(0, 1), (1, 0)]
    share = walk_local // narrow_count
    rows_here = z_count * share
    z_at = lax.axis_index("z")
    wide_at = lax.axis_index(WIDE)
    narrow_at = lax.axis_index(NARROW)
    root_step = math.sqrt(time_step)
    f32, bf16 = jnp.float32, jnp.bfloat16

    packed = packed_cholesky(cholesky)

    offset = comb_source - (wide_at - 1) * walk_local
    chosen = slot_walkers(walkers, offset, wide_count)

    chosen = chosen.reshape(narrow_count, share, row_count, electrons)
    current = dealt(chosen, NARROW)

    own_noise = lax.dynamic_slice_in_dim(noise, narrow_at * share, share, 0)
    own_noise = own_noise.reshape(rows_here, LANES)
    own_offset = lax.dynamic_slice_in_dim(offset, narrow_at * share, share, 0).astype(bf16)
    own_offset = jnp.broadcast_to(own_offset[:, None, None], (share, z_count, LANES))
    side = jnp.concatenate([own_noise, own_offset.reshape(rows_here, LANES)], axis=1)

    rotated = jnp.einsum(
        "wiq,wqp->wpi", walkers, intersection_inverse, preferred_element_type=f32
    ).astype(bf16)
    rotated = rotated.reshape(walk_local, wide_count, -1).transpose(1, 0, 2)
    pairs = exchange(rotated, WIDE)

    y_count, core_count = lax.axis_size("y"), lax.axis_size("c")
    pairs = pairs.reshape(z_count, x_count, y_count, core_count, share, -1)
    pairs = pairs.transpose(3, 1, 2, 0, 4, 5).reshape(core_count, plane_count * rows_here, -1)
    half_flat = half_cholesky.reshape(-1, vectors)
    mine = lax.dynamic_index_in_dim(pairs, core_at, 0, keepdims=False)
    theirs = lax.dynamic_index_in_dim(pairs, 1 - core_at, 0, keepdims=False)
    sent = jnp.dot(theirs, half_flat, preferred_element_type=f32).astype(bf16)
    received = lax.ppermute(sent, "c", swap)
    partial = jnp.dot(mine, half_flat, preferred_element_type=f32) + received.astype(f32)
    partial = partial.astype(bf16).reshape(plane_count, rows_here, vectors)
    partial = exchange(partial, PLANE)

    partial = jnp.sum(partial.astype(f32), axis=0).astype(bf16)
    partial = jnp.concatenate([partial, side], axis=1)
    partial = exchange(jnp.broadcast_to(partial[None], (z_count,) + partial.shape), ("z",))
    bias = jnp.sum(partial[:, :, :vectors].astype(f32), axis=0)
    force_bias = lax.dynamic_slice_in_dim(bias, z_at * share, share, 0)

    noises = partial[:, :, vectors : vectors + LANES].reshape(rows_here, vectors)
    offsets = partial[:, ::z_count, vectors + LANES :].reshape(rows_here, LANES)
    aux = root_step * noises.astype(f32) + time_step * bias
    aux = jnp.concatenate([aux.astype(bf16), offsets], axis=1)
    aux = exchange(jnp.broadcast_to(aux[None], (plane_count,) + aux.shape), PLANE)
    aux = aux.reshape(plane_count * rows_here, vectors + LANES)
    other = lax.ppermute(aux, "c", swap)

    operator = exchange(operator_blocks(core_at, aux, other, packed), MIXED)

    propagated = propagate(narrow_at, operator.transpose(1, 0, 2), current)
    new_walkers = exchange(propagated, NARROW)
    return (new_walkers.reshape(walk_local, row_count, electrons), force_bias)


def solution(mesh):
    fine = Mesh(mesh.devices.reshape(8, 4, 4, 2), ALL)
    in_specs = (
        P(WIDE, NARROW, None),
        P(WIDE, None, None),
        P(WIDE, None),
        P(WIDE, NARROW, None),
        P(NARROW, WIDE, None),
        P(WIDE),
    )
    out_specs = (P(WIDE, NARROW, None), P(ALL, None))

    return jax.shard_map(
        per_device, mesh=fine, in_specs=in_specs, out_specs=out_specs, check_vma=False
    )
```

```python
import math

import jax
import jax.numpy as jnp
from jax import lax
from jax.experimental import pallas as pl
from jax.experimental.pallas import tpu as pltpu
from jax.sharding import Mesh, PartitionSpec as P


time_step = 0.01
WIDE = ("z", "x")
NARROW = ("y", "c")
PLANE = ("x", "y")
MIXED = ("c", "x", "y", "z")
ALL = WIDE + NARROW
LANES = 128


def exchange(blocks, axes):
    return lax.all_to_all(blocks, axes, split_axis=0, concat_axis=0, tiled=True)


def in_vmem(array):
    return pltpu.with_memory_space_constraint(array, pltpu.VMEM)


def in_hbm(array):
    return pltpu.with_memory_space_constraint(array, pltpu.HBM)


def operator_kernel(
    at_ref, own_ref, other_ref, packed_hbm, out_hbm, fields_ref, packed_ref, out_ref, in_sems, out_sems
):
    f32, bf16, i32 = jnp.float32, jnp.bfloat16, jnp.int32
    steps, width, vectors = packed_ref.shape
    rows = own_ref.shape[0]
    core_at = at_ref[0]
    fetches = [
        pltpu.make_async_copy(
            packed_hbm.at[pl.ds(i * width, width), :], packed_ref.at[i], in_sems.at[i]
        )
        for i in range(steps)
    ]
    for fetch in fetches:
        fetch.start()
    slot = lax.broadcasted_iota(i32, (rows, LANES), 0)
    lane = lax.broadcasted_iota(i32, (rows, LANES), 1)
    base = (((slot >> 1) & 7) * 4 + (slot >> 6) - 1) * 16
    tables = (own_ref, other_ref)
    for k, table in enumerate(tables):
        source = table[:, vectors:].astype(f32).astype(i32) + base
        block, inner = source >> 4, source & 15
        row = (((inner >> 1) & 1) ^ core_at) * rows + (block & 3) * 64
        row = row + (inner >> 2) * 16 + (block >> 2) * 2 + (inner & 1)
        fields = jnp.zeros((rows, vectors), f32)
        for half, picked in enumerate(tables):
            hits = [
                (row == lane + (half * rows + at)).astype(f32).astype(bf16)
                for at in range(0, rows, LANES)
            ]
            pick = jnp.concatenate(hits, axis=1)
            fields = fields + jnp.dot(pick, picked[:, :vectors], preferred_element_type=f32)
        fields_ref[k ^ core_at] = fields.astype(bf16)

    writes = []
    for i in range(steps):
        fetches[i].wait()
        for k in range(2):
            product = lax.dot_general(
                fields_ref[k], packed_ref[i], (((1,), (1,)), ((), ())), preferred_element_type=f32
            )
            product = product.astype(bf16).reshape(rows // 2, 2, width)
            out_ref[i, k * (rows // 2) : (k + 1) * (rows // 2)] = product
        write = pltpu.make_async_copy(
            out_ref.at[i], out_hbm.at[:, :, pl.ds(i * width, width)], out_sems.at[i]
        )
        write.start()
        writes.append(write)
    for write in writes:
        write.wait()


def operator_blocks(core_at, own, other, packed):
    rows, _ = own.shape
    columns, vectors = packed.shape
    steps = 2
    width = columns // steps
    whole = pl.BlockSpec(memory_space=pltpu.VMEM)
    anywhere = pl.BlockSpec(memory_space=pltpu.HBM)
    return pl.pallas_call(
        operator_kernel,
        in_specs=[pl.BlockSpec(memory_space=pltpu.SMEM), whole, whole, anywhere],
        out_specs=anywhere,
        out_shape=jax.ShapeDtypeStruct((rows, 2, columns), own.dtype),
        scratch_shapes=[
            pltpu.VMEM((2, rows, vectors), own.dtype),
            pltpu.VMEM((steps, width, vectors), own.dtype),
            pltpu.VMEM((steps, rows, 2, width), own.dtype),
            pltpu.SemaphoreType.DMA((steps,)),
            pltpu.SemaphoreType.DMA((steps,)),
        ],
        compiler_params=pltpu.CompilerParams(vmem_limit_bytes=28 * 2**20),
        name="operator_blocks",
    )(core_at.astype(jnp.int32).reshape(1), in_vmem(own), in_vmem(other), in_hbm(packed))


def dealt(blocks, axes):
    count = lax.axis_size(axes)
    at = lax.axis_index(axes)
    pieces = []
    for k in range(count):
        piece = lax.dynamic_index_in_dim(blocks, at ^ k, 0, keepdims=False)
        if k:
            piece = lax.ppermute(piece, axes, [(i, i ^ k) for i in range(count)])
        pieces.append(piece)
    return pieces


def slot_walkers(walkers, offset, wide_count):
    up = [(i, (i + 1) % wide_count) for i in range(wide_count - 1)]
    down = [(j, i) for i, j in up]
    before = lax.ppermute(walkers, WIDE, up)
    after = lax.ppermute(walkers, WIDE, down)
    padded = jnp.concatenate([before, walkers, after], axis=0)
    return jnp.take(padded, offset, axis=0)


def pack_kernel(chol_ref, out_ref, wide_ref):
    row_count, col_count, width = chol_ref.shape
    f32, bf16 = jnp.float32, jnp.bfloat16
    full = out_ref.shape[0]
    for at in range(0, width, LANES):
        wide_ref[...] = chol_ref[:, :, at : at + LANES].astype(f32).reshape(row_count * col_count, LANES)
        for j in range(full):
            out_ref[j, :row_count, at : at + LANES] = wide_ref[pl.ds(j, row_count, stride=col_count), :].astype(bf16)
        for j in range(full, col_count):
            column = wide_ref[pl.ds(j, row_count, stride=col_count), :].astype(bf16)
            for p in range(3):
                out_ref[3 * (j - full) + p, row_count:, at : at + LANES] = column[p * 32 : (p + 1) * 32]


def packed_cholesky(cholesky):
    row_count, col_count, vectors = cholesky.shape
    full = col_count * row_count // LANES
    width = 256
    packed = pl.pallas_call(
        pack_kernel,
        grid=(vectors // width,),
        in_specs=[pl.BlockSpec((row_count, col_count, width), lambda i: (0, 0, i))],
        out_specs=pl.BlockSpec((full, LANES, width), lambda i: (0, 0, i)),
        out_shape=jax.ShapeDtypeStruct((full, LANES, vectors), cholesky.dtype),
        scratch_shapes=[pltpu.VMEM((row_count * col_count, LANES), jnp.float32)],
        name="pack",
    )(cholesky)
    return packed.reshape(full * LANES, vectors)


def propagate_kernel(at_ref, blocks_ref, *refs):
    *current_refs, out_ref, matrix_ref, term_ref, total_ref = refs
    share = blocks_ref.shape[0]
    f32, bf16 = jnp.float32, jnp.bfloat16
    lane = lax.broadcasted_iota(jnp.int32, (32, 128), 1)

    def assemble(s):
        def rows_of(t, n):
            at = t * 128
            first = (n & 1) * 128 + (n >> 1) * 8
            pieces = [
                blocks_ref[s, first + x * 32 : first + x * 32 + 8, at : at + 128]
                for x in range(4)
            ]
            return jnp.concatenate([piece.astype(f32) for piece in pieces], axis=0)

        for j in range(24):
            chunks = []
            for n in range(8):
                if j < 18:
                    chunk = rows_of(j, n)
                else:
                    q = 3 * (j - 18)
                    chunk = jnp.where(
                        lane < 32,
                        pltpu.roll(rows_of(q, n), 32, 1),
                        jnp.where(
                            lane < 64,
                            pltpu.roll(rows_of(q + 1, n), 64, 1),
                            pltpu.roll(rows_of(q + 2, n), 96, 1),
                        ),
                    )
                chunks.append(chunk)
            for half in range(2):
                first, second, third, fourth = chunks[4 * half : 4 * half + 4]
                second = pltpu.roll(second, 96, 1)
                third = pltpu.roll(third, 64, 1)
                fourth = pltpu.roll(fourth, 32, 1)
                tiles = (
                    jnp.where(lane < 96, first, second),
                    jnp.where(lane < 64, second, third),
                    jnp.where(lane < 32, third, fourth),
                )
                for k, tile in enumerate(tiles):
                    at = half * 384 + k * 128
                    matrix_ref[s, j * 32 : (j + 1) * 32, at : at + 128] = tile.astype(bf16)

    for s in range(share):
        assemble(s)
    narrow, _, rows_each, _ = out_ref.shape
    for k, current_ref in enumerate(current_refs):
        first_row = pl.multiple_of((at_ref[0] ^ k) * rows_each, 8)
        for s in range(share):
            start = current_ref[s].astype(f32)
            term_ref[s, pl.ds(first_row, rows_each), :] = start
            total_ref[s, pl.ds(first_row, rows_each), :] = start
    for degree in range(1, 5):
        for s in range(share):
            rows = [
                term_ref[s, pl.ds(x * 24 + j, 8, stride=96), :]
                for j in range(24)
                for x in range(4)
            ]
            ordered = jnp.concatenate(rows, axis=0).astype(bf16)
            product = lax.dot_general(
                ordered, matrix_ref[s], (((0,), (0,)), ((), ())), preferred_element_type=f32
            )
            product = product.T * (1.0 / degree)
            if degree < 4:
                product = product.astype(bf16).astype(f32)
                term_ref[s] = product
                total_ref[s] = total_ref[s] + product
            else:
                product = (total_ref[s] + product).astype(bf16)
                for n in range(narrow):
                    out_ref[n, s] = product[n * rows_each : (n + 1) * rows_each]


def propagate(narrow_at, blocks, current):
    narrow = len(current)
    share, rows_each, electrons = current[0].shape
    orbitals = narrow * rows_each
    f32, bf16 = jnp.float32, jnp.bfloat16
    whole = pl.BlockSpec(memory_space=pltpu.VMEM)
    return pl.pallas_call(
        propagate_kernel,
        in_specs=[pl.BlockSpec(memory_space=pltpu.SMEM)] + [whole] * (1 + narrow),
        out_specs=whole,
        out_shape=pltpu.VMEM((narrow, share, rows_each, electrons), bf16),
        scratch_shapes=[
            pltpu.VMEM((share, orbitals, orbitals), bf16),
            pltpu.VMEM((share, orbitals, electrons), f32),
            pltpu.VMEM((share, orbitals, electrons), f32),
        ],
        compiler_params=pltpu.CompilerParams(vmem_limit_bytes=24 * 2**20),
        name="propagate",
    )(narrow_at.astype(jnp.int32).reshape(1), in_vmem(blocks), *map(in_vmem, current))


def per_device(walkers, intersection_inverse, noise, half_cholesky, cholesky, comb_source):
    walk_local, row_count, electrons = walkers.shape
    vectors = cholesky.shape[2]
    z_count, x_count = lax.axis_size("z"), lax.axis_size("x")
    wide_count = z_count * x_count
    narrow_count = lax.axis_size(NARROW)
    plane_count = lax.axis_size(PLANE)
    core_at = lax.axis_index("c")
    swap = [(0, 1), (1, 0)]
    share = walk_local // narrow_count
    rows_here = z_count * share
    z_at = lax.axis_index("z")
    wide_at = lax.axis_index(WIDE)
    narrow_at = lax.axis_index(NARROW)
    root_step = math.sqrt(time_step)
    f32, bf16 = jnp.float32, jnp.bfloat16

    packed = packed_cholesky(cholesky)

    offset = comb_source - (wide_at - 1) * walk_local
    chosen = slot_walkers(walkers, offset, wide_count)

    chosen = chosen.reshape(narrow_count, share, row_count, electrons)
    current = dealt(chosen, NARROW)

    own_noise = lax.dynamic_slice_in_dim(noise, narrow_at * share, share, 0)
    own_noise = own_noise.reshape(rows_here, LANES)
    own_offset = lax.dynamic_slice_in_dim(offset, narrow_at * share, share, 0).astype(bf16)
    own_offset = jnp.broadcast_to(own_offset[:, None, None], (share, z_count, LANES))
    side = jnp.concatenate([own_noise, own_offset.reshape(rows_here, LANES)], axis=1)

    rotated = jnp.einsum(
        "wiq,wqp->wpi", walkers, intersection_inverse, preferred_element_type=f32
    ).astype(bf16)
    rotated = rotated.reshape(walk_local, wide_count, -1).transpose(1, 0, 2)
    pairs = exchange(rotated, WIDE)

    y_count, core_count = lax.axis_size("y"), lax.axis_size("c")
    pairs = pairs.reshape(z_count, x_count, y_count, core_count, share, -1)
    pairs = pairs.transpose(3, 1, 2, 0, 4, 5).reshape(core_count, plane_count * rows_here, -1)
    half_flat = half_cholesky.reshape(-1, vectors)
    theirs = lax.dynamic_index_in_dim(pairs, 1 - core_at, 0, keepdims=False)
    sent = jnp.dot(theirs, half_flat, preferred_element_type=f32).astype(bf16)
    pairs, sent = lax.optimization_barrier((pairs, sent))
    received = lax.ppermute(sent, "c", swap)
    mine = lax.dynamic_index_in_dim(pairs, core_at, 0, keepdims=False)
    own = jnp.dot(mine, half_flat, preferred_element_type=f32)
    own = lax.optimization_barrier(own)
    partial = own + received.astype(f32)
    partial = partial.astype(bf16).reshape(plane_count, rows_here, vectors)
    partial = exchange(partial, PLANE)

    partial = jnp.sum(partial.astype(f32), axis=0).astype(bf16)
    partial = jnp.concatenate([partial, side], axis=1)
    partial = exchange(jnp.broadcast_to(partial[None], (z_count,) + partial.shape), ("z",))
    bias = jnp.sum(partial[:, :, :vectors].astype(f32), axis=0)
    force_bias = lax.dynamic_slice_in_dim(bias, z_at * share, share, 0)

    noises = partial[:, :, vectors : vectors + LANES].reshape(rows_here, vectors)
    offsets = partial[:, ::z_count, vectors + LANES :].reshape(rows_here, LANES)
    aux = root_step * noises.astype(f32) + time_step * bias
    aux = jnp.concatenate([aux.astype(bf16), offsets], axis=1)
    aux = exchange(jnp.broadcast_to(aux[None], (plane_count,) + aux.shape), PLANE)
    aux = aux.reshape(plane_count * rows_here, vectors + LANES)
    other = lax.ppermute(aux, "c", swap)

    operator = exchange(operator_blocks(core_at, aux, other, packed), MIXED)

    propagated = propagate(narrow_at, operator.transpose(1, 0, 2), current)
    new_walkers = exchange(propagated, NARROW)
    return (new_walkers.reshape(walk_local, row_count, electrons), force_bias)


def solution(mesh):
    fine = Mesh(mesh.devices.reshape(8, 4, 4, 2), ALL)
    in_specs = (
        P(WIDE, NARROW, None),
        P(WIDE, None, None),
        P(WIDE, None),
        P(WIDE, NARROW, None),
        P(NARROW, WIDE, None),
        P(WIDE),
    )
    out_specs = (P(WIDE, NARROW, None), P(ALL, None))

    return jax.shard_map(
        per_device, mesh=fine, in_specs=in_specs, out_specs=out_specs, check_vma=False
    )
```
